32 devices in a mesh: groups: 2 (over y), rows: 4 (over z), cols: 2 (over x), chan: 2 (over core).
Axes of the slice: x: 2, y: 2, z: 4, core: 2. Of those that a mesh axis runs over, the one named last changes fastest.
Arguments:
- patches: bfloat16 [128, 16, 1024], P(('groups', 'rows'), 'cols', 'chan'), parts along dimension 0, may hold values from -6 to 6
- steps: float32 [128, 16, 1024], P(('groups', 'rows'), 'cols', 'chan'), parts along dimension 0, may hold values from 0.1 to 1
- decay_codes: int32 [128, 16], P(('groups', 'rows'), 'cols'), parts along dimension 0, may hold values from 0 to 15
- tissue_mask: int32 [128, 16], P(('groups', 'rows'), 'cols'), parts along dimension 0, may hold values 0 or 1
- decay_rates: float32 [16, 1024], P(None, 'chan'), may hold values from 0.002 to 4
- input_map: float32 [128, 16, 16], P(('groups', 'rows'), 'cols'), parts along dimension 0, may hold values from -1.5 to 1.5
- output_map: float32 [128, 16, 16], P(('groups', 'rows'), 'cols'), parts along dimension 0, may hold values from -1.5 to 1.5
- out_grad: bfloat16 [128, 16, 1024], P(('groups', 'rows'), 'cols', 'chan'), parts along dimension 0, may hold values from -0.59765625 to 0.59765625
Outputs:
- patches_grad: bfloat16 [128, 16, 1024], P(('groups', 'rows'), 'cols', 'chan'), parts along dimension 0
- steps_grad: float32 [128, 16, 1024], P(('groups', 'rows'), 'cols', 'chan'), parts along dimension 0
- input_map_grad: float32 [128, 16, 16], P(('groups', 'rows'), 'cols'), parts along dimension 0
- output_map_grad: float32 [128, 16, 16], P(('groups', 'rows'), 'cols'), parts along dimension 0
The draws below stay inside these ranges and needn't reach their ends.
There are 2 independent parts, one for each index of `groups`. The reference program is written for one: setup_inputs(seed, part) draws one part's arguments, and reference() takes and returns one part's arrays. A program takes and returns all parts, laid end to end along the dimension named above; an argument that names none is the same for every part. Nothing has to cross between parts.
Inputs may be any that keep to these rules, and one draw needn't show every extreme that they name: `decay_codes`: a decay code of each patch.
All inputs are finite; a program needn't handle non-finite values. No bound on the sum of `tissue_mask` on one device may be relied on, other than what follows from the above.
Results may differ from the reference program's by a relative error of at most 0.0014.
Values sent between devices are 32-bit elements; how exact they have to be, the bound alone decides.
No kernel may reach another device: no remote copies, remote signals or barrier semaphores. Data moves between devices by JAX's collectives and lax.ppermute only.
A program may use at most 128 MiB of HBM per device.

```python
import math
import jax
import jax.numpy as jnp
from jax import lax

D = 1024
STATES = 16
CODES = 16
NR = 64
NC = 16


def place_ends(result, key, low, top_value):
    index_at = [jax.random.randint(jax.random.fold_in(key, axis), (), 0, length) for axis, length in enumerate(result.shape)]
    widest = result.shape.index(max(result.shape))
    next_to = index_at[:widest] + [(index_at[widest] + 1) % result.shape[widest]] + index_at[widest + 1:]
    return result.at[tuple(index_at)].set(low).at[tuple(next_to)].set(top_value)


def steps_of(own_key, shape, cuts, least, largest):
    gain = 1.0
    for position, blocks in cuts:
        draws = jax.random.uniform(jax.random.fold_in(jax.random.fold_in(own_key, 6), position), (blocks,), jnp.float32, least / len(cuts), largest / len(cuts))
        gain = gain * jnp.repeat(jnp.exp(draws), shape[position] // blocks).reshape((-1,) + (1,) * (len(shape) - 1 - position))
    return gain


def normal_values(stream_key, shape, scale, reach, cuts=(), dtype=jnp.bfloat16):
    result = jax.random.normal(stream_key, shape, jnp.float32) * scale
    if len(cuts) > 0:
        result = steps_of(stream_key, shape, cuts, -0.22, 0.18) * result
    return jnp.clip(result, min=-reach, max=reach).astype(dtype)


def setup_inputs(seed: int = 0, part: int = 0) -> dict:
    key_of = jax.random.split(jax.random.key(seed), 9)
    part_splits = jax.random.split(jax.random.fold_in(key_of[8], part), 9)
    patches = normal_values(part_splits[0], (NR, NC, D), 1.0, 6.0, ((0, 4), (1, 2), (2, 2)))
    steps = jnp.clip(jnp.exp(math.log(1.0) - 2.3025851 * jax.random.uniform(part_splits[1], (NR, NC, D), jnp.float32) ** steps_of(part_splits[1], (NR, NC, D), ((0, 4), (1, 2), (2, 2)), -0.2, 0.2)), 0.1, 1.0)
    decay_codes = place_ends(jax.random.randint(part_splits[2], (NR, NC), 0, CODES), jax.random.fold_in(part_splits[2], 1), 0, CODES - 1).astype(jnp.int32)
    tissue_mask = place_ends((jax.random.randint(part_splits[3], (NR, NC), 0, 4) < 3).astype(jnp.int32), jax.random.fold_in(part_splits[3], 1), 0, 1)
    decay_rates = jnp.clip(jnp.exp(math.log(4.0) - 7.6009024 * jax.random.uniform(key_of[4], (STATES, D), jnp.float32) ** steps_of(key_of[4], (STATES, D), ((1, 2),), -0.2, 0.2)), 0.002, 4.0)
    input_map = normal_values(part_splits[5], (NR, NC, STATES), 0.25, 1.5, ((0, 4), (1, 2)), jnp.float32)
    output_map = normal_values(part_splits[6], (NR, NC, STATES), 0.25, 1.5, ((0, 4), (1, 2)), jnp.float32)
    out_grad = normal_values(part_splits[7], (NR, NC, D), 0.1, 0.59765625, ((0, 4), (1, 2), (2, 2)))
    return {"patches": patches, "steps": steps, "decay_codes": decay_codes, "tissue_mask": tissue_mask, "decay_rates": decay_rates, "input_map": input_map, "output_map": output_map, "out_grad": out_grad}


def pair_combine(first, second):
    return (first[0] * second[0], second[0] * first[1] + second[1])


def block_grads(patches, steps, keep, maskf, rates, input_map, output_map, out_grad):
    xf = patches.astype(jnp.float32)
    gyf = out_grad.astype(jnp.float32)
    decay = jnp.exp(keep[:, :, None, None] * rates[None, None] * steps[:, :, None, :])
    drive = maskf[:, :, None] * steps * xf
    source = input_map[:, :, :, None] * drive[:, :, None, :]
    _, row_state = lax.associative_scan(pair_combine, (decay, source), axis=1)
    _, state = lax.associative_scan(pair_combine, (decay, row_state), axis=0)
    state_cot = output_map[:, :, :, None] * gyf[:, :, None, :]
    below = jnp.concatenate([decay[1:], jnp.ones_like(decay[:1])], axis=0)
    _, col_cot = lax.associative_scan(pair_combine, (below, state_cot), axis=0, reverse=True)
    right = jnp.concatenate([decay[:, 1:], jnp.ones_like(decay[:, :1])], axis=1)
    _, row_cot = lax.associative_scan(pair_combine, (right, col_cot), axis=1, reverse=True)
    above_state = jnp.concatenate([jnp.zeros_like(state[:1]), state[:-1]], axis=0)
    left_state = jnp.concatenate([jnp.zeros_like(row_state[:, :1]), row_state[:, :-1]], axis=1)
    decay_cot = decay * (col_cot * above_state + row_cot * left_state)
    drive_cot = jnp.sum(row_cot * input_map[:, :, :, None], axis=2)
    patches_grad = (drive_cot * maskf[:, :, None] * steps).astype(jnp.bfloat16)
    steps_grad = drive_cot * maskf[:, :, None] * xf + jnp.sum(decay_cot * keep[:, :, None, None] * rates[None, None], axis=2)
    map_in = jnp.sum(row_cot * drive[:, :, None, :], axis=3)
    map_out = jnp.sum(gyf[:, :, None, :] * state, axis=3)
    return patches_grad, steps_grad, map_in, map_out


def reference(patches, steps, decay_codes, tissue_mask, decay_rates, input_map, output_map, out_grad):
    maskf = tissue_mask.astype(jnp.float32)
    levels = 0.7 + 0.25 * decay_codes.astype(jnp.float32) / (CODES - 1)
    keep = maskf * jnp.log(levels)
    width = math.gcd(D, 128)
    count = D // width

    def split(field):
        return jnp.moveaxis(field.reshape(NR, NC, count, width), 2, 0)

    rate_blocks = jnp.moveaxis(decay_rates.reshape(STATES, count, width), 1, 0)

    def one_block(carry, pieces):
        xb, sb, rb, gb = pieces
        pg, sg, mi, mo = block_grads(xb, sb, keep, maskf, rb, input_map, output_map, gb)
        return (carry[0] + mi, carry[1] + mo), (pg, sg)

    zeros = jnp.zeros((NR, NC, STATES), jnp.float32)
    sums, grads = lax.scan(one_block, (zeros, zeros), (split(patches), split(steps), rate_blocks, split(out_grad)))

    def join(blocks):
        return jnp.moveaxis(blocks, 0, 2).reshape(NR, NC, D)

    return join(grads[0]), join(grads[1]), sums[0], sums[1]
```

```python
import functools
import math
import jax
import jax.numpy as jnp
from jax import lax
from jax.experimental import pallas as pl
from jax.experimental.pallas import tpu as pltpu
from jax.sharding import PartitionSpec as P

CODES = 16
CHUNKS = 1
LOG2E = 1.4426950408889634
f32 = jnp.float32


def call(body, outs, scratch, name, args):
    vmem = pl.BlockSpec(memory_space=pltpu.VMEM)
    return pl.pallas_call(
        body,
        out_shape=tuple(outs),
        in_specs=[vmem] * len(args),
        out_specs=tuple([vmem] * len(outs)),
        scratch_shapes=scratch,
        name=name,
    )(*args)


def column_of(row, eye):
    return jnp.sum(jnp.where(eye, jnp.broadcast_to(row, eye.shape), 0.0), axis=1, keepdims=True)


def spread_map(map_ref, wide_ref):
    rows, cols, n = map_ref.shape
    turned = jnp.transpose(map_ref[...].reshape(rows * cols, n))
    for p in range(rows * cols):
        wide_ref[p] = jnp.broadcast_to(turned[:, p : p + 1], (n, 128))


def widen(tile, width):
    return jnp.concatenate([tile] * (width // 128), axis=1)


def prepare(steps_ref, patches_ref, codes_ref, mask_ref, log_ref, drive_ref, ms_ref, mx_ref, keep_ref):
    rows, cols, _ = steps_ref.shape
    maskf = mask_ref[...].astype(f32)
    keep = maskf * jnp.log(0.7 + 0.25 * codes_ref[...].astype(f32) / (CODES - 1))
    eye = lax.broadcasted_iota(jnp.int32, (cols, cols), 0) == lax.broadcasted_iota(jnp.int32, (cols, cols), 1)
    for i in range(rows):
        kept = column_of(keep[i : i + 1, :], eye)
        masked = column_of(maskf[i : i + 1, :], eye)
        step = steps_ref[i]
        x = patches_ref[i].astype(f32)
        masked_step = masked * step
        log_ref[i] = (kept * LOG2E) * step
        drive_ref[i] = masked_step * x
        ms_ref[i] = masked_step
        mx_ref[i] = masked * x
        keep_ref[i] = jnp.broadcast_to(kept, (cols, 128))


def row_ends(span, log_ref, drive_ref, rates_ref, in_ref, off_ref):
    rows, cols, _ = log_ref.shape
    lo, width = span
    lanes = pl.ds(lo, width)

    def one_row(i, _):
        rates = rates_ref[:, lanes]
        carry = None
        for j in range(cols):
            source = widen(in_ref[i * cols + j], width) * drive_ref[i, j : j + 1, lanes]
            if carry is None:
                carry = source
            else:
                carry = jnp.exp2(rates * log_ref[i, j : j + 1, lanes]) * carry + source
        off_ref[i] = carry
        return 0

    lax.fori_loop(0, rows, one_row, 0)


def first_rows(span, steps_ref, patches_ref, codes_ref, mask_ref, rates_ref, map_ref,
               off_ref, log_ref, drive_ref, ms_ref, mx_ref, keep_ref, in_ref):
    prepare(steps_ref, patches_ref, codes_ref, mask_ref, log_ref, drive_ref, ms_ref, mx_ref, keep_ref)
    spread_map(map_ref, in_ref)
    row_ends(span, log_ref, drive_ref, rates_ref, in_ref, off_ref)


def more_rows(span, log_ref, drive_ref, rates_ref, in_ref, off_ref):
    row_ends(span, log_ref, drive_ref, rates_ref, in_ref, off_ref)


def col_starts(span, log_ref, grad_ref, rates_ref, out_ref, off_ref, factor_ref):
    rows, cols, _ = log_ref.shape
    lo, width = span
    lanes = pl.ds(lo, width)
    for j in range(cols):
        off_ref[j] = jnp.zeros(off_ref.shape[1:], f32)

    def one_row(turn, _):
        i = rows - 1 - turn
        rates = rates_ref[:, lanes]
        for j in range(cols):
            cot = widen(out_ref[i * cols + j], width) * grad_ref[i, j : j + 1, lanes] + off_ref[j]
            off_ref[j] = jnp.exp2(rates * log_ref[i, j : j + 1, lanes]) * cot
        return 0

    lax.fori_loop(0, rows, one_row, 0)
    total = log_ref[0, :, lanes]
    for i in range(1, rows):
        total = total + log_ref[i, :, lanes]
    rates = rates_ref[:, lanes]
    for j in range(cols):
        factor_ref[j] = jnp.exp2(rates * total[j : j + 1])


def first_cols(span, log_ref, out_grad_ref, rates_ref, map_ref, off_ref, factor_ref, grad_ref, out_ref):
    for i in range(log_ref.shape[0]):
        grad_ref[i] = out_grad_ref[i].astype(f32)
    spread_map(map_ref, out_ref)
    col_starts(span, log_ref, grad_ref, rates_ref, out_ref, off_ref, factor_ref)


def more_cols(span, log_ref, grad_ref, rates_ref, out_ref, off_ref, factor_ref):
    col_starts(span, log_ref, grad_ref, rates_ref, out_ref, off_ref, factor_ref)


def forward(span, log_ref, drive_ref, rates_ref, in_ref, left_ref, row_ref, off_ref):
    rows, cols, _ = log_ref.shape
    lo, width = span
    lanes = pl.ds(lo, width)
    for j in range(cols):
        off_ref[j] = jnp.zeros(off_ref.shape[1:], f32)

    def one_row(i, _):
        rates = rates_ref[:, lanes]
        carry = left_ref[i]
        for j in range(cols):
            factor = jnp.exp2(rates * log_ref[i, j : j + 1, lanes])
            carry = factor * carry + widen(in_ref[i * cols + j], width) * drive_ref[i, j : j + 1, lanes]
            row_ref[i * cols + j] = carry
            off_ref[j] = factor * off_ref[j] + carry
        return 0

    lax.fori_loop(0, rows, one_row, 0)


def backward(span, log_ref, grad_ref, rates_ref, out_ref, bottom_ref, col_ref, off_ref, carry_ref):
    rows, cols, _ = log_ref.shape
    lo, width = span
    lanes = pl.ds(lo, width)
    for j in range(cols):
        carry_ref[j] = bottom_ref[j]

    def one_row(turn, _):
        i = rows - 1 - turn
        rates = rates_ref[:, lanes]
        lead = None
        for j in reversed(range(cols)):
            factor = jnp.exp2(rates * log_ref[i, j : j + 1, lanes])
            cot = widen(out_ref[i * cols + j], width) * grad_ref[i, j : j + 1, lanes] + carry_ref[j]
            col_ref[i * cols + j] = cot
            carry_ref[j] = factor * cot
            lead = factor * (cot if lead is None else cot + lead)
        off_ref[i] = lead
        return 0

    lax.fori_loop(0, rows, one_row, 0)


def finish(span, log_ref, drive_ref, grad_ref, rates_ref, in_ref, row_ref, col_ref, ms_ref, mx_ref, keep_ref,
           left_ref, top_ref, right_ref, *refs):
    chained = len(refs) == 9
    if chained:
        before_ref, gx_ref, gs_ref, maps_ref, carry_ref, drive_cot_ref, log_cot_ref = refs[0], *refs[3:]
    else:
        gx_ref, gs_ref, maps_ref, carry_ref, drive_cot_ref, log_cot_ref = refs
    rows, cols, _ = log_ref.shape
    n = rates_ref.shape[0]
    lo, width = span
    lanes = pl.ds(lo, width)
    for j in range(cols):
        carry_ref[j] = top_ref[j]
    spot = lax.broadcasted_iota(jnp.int32, (n, rows * cols), 1)

    def one_row(i, sums):
        map_in, map_out = sums
        rates = rates_ref[:, lanes]
        lead = right_ref[i]
        here = row_ref[i * cols + cols - 1]
        for j in reversed(range(cols)):
            p = i * cols + j
            left = row_ref[p - 1] if j > 0 else left_ref[i]
            factor = jnp.exp2(rates * log_ref[i, j : j + 1, lanes])
            above = carry_ref[j]
            state = factor * above + here
            carry_ref[j] = state
            col_cot = col_ref[p]
            row_cot = col_cot + lead
            lead = factor * row_cot
            log_cot = (col_cot * (factor * above) + lead * left) * rates
            drive_cot = row_cot * widen(in_ref[p], width)
            drive_cot_ref[j : j + 1, :] = jnp.sum(drive_cot, axis=0, keepdims=True)
            log_cot_ref[j : j + 1, :] = jnp.sum(log_cot, axis=0, keepdims=True)
            at = spot == p
            map_in = jnp.where(at, jnp.sum(row_cot * drive_ref[i, j : j + 1, lanes], axis=1, keepdims=True), map_in)
            map_out = jnp.where(at, jnp.sum(state * grad_ref[i, j : j + 1, lanes], axis=1, keepdims=True), map_out)
            here = left
        drive_cot = drive_cot_ref[...]
        gx_ref[i, :, lanes] = (drive_cot * ms_ref[i, :, lanes]).astype(jnp.bfloat16)
        gs_ref[i, :, lanes] = drive_cot * mx_ref[i, :, lanes] + log_cot_ref[...] * widen(keep_ref[i], width)
        return map_in, map_out

    zero = jnp.zeros((n, rows * cols), f32)
    start = (before_ref[0:n, :], before_ref[n:, :]) if chained else (zero, zero)
    map_in, map_out = lax.fori_loop(0, rows, one_row, start)
    maps_ref[0:n, :] = map_in
    maps_ref[n:, :] = map_out


def sd(*shape, dtype=f32):
    return jax.ShapeDtypeStruct(shape, dtype)


def relay(offset, factor, axis, forwards):
    size = lax.axis_size(axis)
    entering = None
    for turn in range(size - 1):
        route = [(turn, turn + 1)] if forwards else [(size - 1 - turn, size - 2 - turn)]
        sent = offset if entering is None else factor * entering + offset
        got = lax.ppermute(sent, axis, route)
        entering = got if entering is None else entering + got
    return jnp.zeros_like(offset) if entering is None else entering


def local(patches, steps, decay_codes, tissue_mask, decay_rates, input_map, output_map, out_grad):
    rows, cols, width = steps.shape
    n = decay_rates.shape[0]
    part = width // CHUNKS
    spans = [(k * part, part) for k in range(CHUNKS)]
    places = rows * cols
    field = sd(places, n, part)
    row_edge = sd(rows, n, part)
    col_edge = sd(cols, n, part)
    whole = sd(rows, cols, width)

    row_offs, col_offs, col_factors = [], [], []
    for k, span in enumerate(spans):
        tag = "_" + str(k)
        if k == 0:
            off, log, drive, ms, mx, keep, in_wide = call(
                functools.partial(first_rows, span),
                [row_edge, whole, whole, whole, whole, sd(rows, cols, 128), sd(places, n, 128)],
                [], "row_ends" + tag,
                (steps, patches, decay_codes, tissue_mask, decay_rates, input_map),
            )
        else:
            (off,) = call(functools.partial(more_rows, span), [row_edge], [], "row_ends" + tag,
                          (log, drive, decay_rates, in_wide))
        row_offs.append(off)
        if k == 0:
            off, factor, grad, out_wide = call(
                functools.partial(first_cols, span),
                [col_edge, col_edge, whole, sd(places, n, 128)],
                [], "col_starts" + tag,
                (log, out_grad, decay_rates, output_map),
            )
        else:
            off, factor = call(functools.partial(more_cols, span), [col_edge, col_edge], [], "col_starts" + tag,
                               (log, grad, decay_rates, out_wide))
        col_offs.append(off)
        col_factors.append(factor)

    many = lax.axis_size("cols") > 2
    row_total = jnp.sum(log, axis=1)
    lefts, tops, bottoms, rights, fields, cots = [], [], [], [], [], []
    for k, span in enumerate(spans):
        lo = span[0]
        row_factor = None
        if many:
            row_factor = jnp.exp2(row_total[:, None, lo : lo + part] * decay_rates[None, :, lo : lo + part])
        left = relay(row_offs[k], row_factor, "cols", True)
        bottom = relay(col_offs[k], col_factors[k], "rows", False)
        row_field, down = call(functools.partial(forward, span), [field, col_edge], [], "forward_" + str(k),
                               (log, drive, decay_rates, in_wide, left))
        top = relay(down, col_factors[k], "rows", True)
        col_field, lead = call(functools.partial(backward, span), [field, row_edge],
                               [pltpu.VMEM((cols, n, part), f32)], "backward_" + str(k),
                               (log, grad, decay_rates, out_wide, bottom))
        right = relay(lead, row_factor, "cols", False)
        lefts.append(left)
        tops.append(top)
        rights.append(right)
        fields.append(row_field)
        cots.append(col_field)

    maps = None
    for k, span in enumerate(spans):
        args = [log, drive, grad, decay_rates, in_wide, fields[k], cots[k], ms, mx, keep, lefts[k], tops[k], rights[k]]
        aliases = {}
        if maps is not None:
            args += [maps, gx, gs]
            aliases = {len(args) - 2: 0, len(args) - 1: 1}
        vmem = pl.BlockSpec(memory_space=pltpu.VMEM)
        gx, gs, maps = pl.pallas_call(
            functools.partial(finish, span),
            out_shape=(sd(rows, cols, width, dtype=jnp.bfloat16), whole, sd(2 * n, places)),
            in_specs=[vmem] * len(args),
            out_specs=(vmem, vmem, vmem),
            scratch_shapes=[pltpu.VMEM((cols, n, part), f32), pltpu.VMEM((cols, part), f32), pltpu.VMEM((cols, part), f32)],
            input_output_aliases=aliases,
            name="finish_" + str(k),
        )(*args)

    if lax.axis_size("chan") == 2:
        maps = maps + lax.ppermute(maps, "chan", [(0, 1), (1, 0)])
    else:
        maps = lax.psum(maps, "chan")
    turned = jnp.transpose(maps).reshape(rows, cols, 2 * n)
    return gx, gs, turned[:, :, :n], turned[:, :, n:]


def solution(mesh):
    in_specs = (
        P(("groups", "rows"), "cols", "chan"),
        P(("groups", "rows"), "cols", "chan"),
        P(("groups", "rows"), "cols"),
        P(("groups", "rows"), "cols"),
        P(None, "chan"),
        P(("groups", "rows"), "cols", None),
        P(("groups", "rows"), "cols", None),
        P(("groups", "rows"), "cols", "chan"),
    )
    out_specs = (
        P(("groups", "rows"), "cols", "chan"),
        P(("groups", "rows"), "cols", "chan"),
        P(("groups", "rows"), "cols", None),
        P(("groups", "rows"), "cols", None),
    )
    return jax.shard_map(local, mesh=mesh, in_specs=in_specs, out_specs=out_specs, check_vma=False)
```
